32 devices in a mesh: grp: 8 (over z, y), rep: 2 (over core), tp: 2 (over x).
Axes of the slice: x: 2, y: 2, z: 4, core: 2. Of those that a mesh axis runs over, the one named last changes fastest.
Arguments:
- hidden: bfloat16 [8, 768, 8192], P('grp', 'rep'), may hold values from -6 to 6
- decode_hidden: bfloat16 [8, 2, 2, 32, 8192], P('grp', 'rep'), may hold values from -6 to 6
- norm_gain: bfloat16 [8192], replicated, may hold values from 0.25 to 1.75
- qkv_weight: bfloat16 [8192, 10240], P('grp', 'tp'), may hold values from -0.0625 to 0.0625
- qkv_bias: bfloat16 [10240], P('tp'), may hold values from -32 to 32
- lengths: int32 [8], replicated, may hold values from 12 to 768, as said below
Outputs:
- prefill_out: bfloat16 [8, 768, 8192], P('grp', 'rep', 'tp')
- decode_out: bfloat16 [8, 2, 2, 32, 8192], P('grp', 'rep', None, None, 'tp')
The draws below stay inside these ranges and needn't reach their ends.
Inputs may be any that keep to these rules, and one draw needn't show every extreme that they name: `lengths`: some prompt is 768 tokens long.
All inputs are finite; a program needn't handle non-finite values.
Results may differ from the reference program's by a relative error of at most 0.012.
The reference program's roundings to bfloat16 on the way count: a program that leaves them out, or rounds other values in their place, can miss the bound.
Values may be sent and summed in bfloat16 or wider, within the bound.
A program may use at most 256 MiB of HBM per device.

```python
import jax
import jax.numpy as jnp
from jax import lax

D = 8192
KVH = 8
HD = 128
QPK = 8
PROMPT = 768
SAMP = 8
STEPS = 4
PROMPTS = 8
N_REP = 2


def draw_qkv_bias(key, part):
    base_bias = jnp.clip(jax.random.normal(jax.random.fold_in(key, 11), (KVH, QPK + 2, HD), jnp.float32), -4.0, 4.0) * 0.5
    return base_bias.reshape(KVH * (QPK + 2) * HD).astype(jnp.bfloat16)


def draw_lengths(key, part):
    shortest = max(1, PROMPT // 64)
    random_lengths = jax.random.randint(jax.random.fold_in(key, 21), (PROMPTS,), shortest, PROMPT + 1)
    longest = jax.random.randint(jax.random.fold_in(key, 22), (), 0, PROMPTS)
    return jnp.where(jnp.arange(PROMPTS) == longest, PROMPT, random_lengths).astype(jnp.int32)


def levels(stream_key, dims, pieces, low, largest):
    level, own = 1.0, jax.random.fold_in(stream_key, 6)
    for dim, parts in pieces:
        heights = jnp.exp(jax.random.uniform(jax.random.fold_in(own, dim), (parts,), jnp.float32, low / len(pieces), largest / len(pieces)))
        level = level * jnp.repeat(heights, dims[dim] // parts).reshape([-1 if axis == dim else 1 for axis in range(len(dims))])
    return level


def gaussian(key, dims, width, reach, pieces=(), held_as=jnp.bfloat16):
    values = jax.random.normal(key, dims, jnp.float32) * width
    if len(pieces) > 0:
        values = levels(key, dims, pieces, -0.22, 0.18) * values
    return jnp.clip(values, min=-reach, max=reach).astype(held_as)


def setup_inputs(seed: int = 0) -> dict:
    seeds = jax.random.split(jax.random.key(seed), 7)
    hidden = gaussian(seeds[0], (PROMPTS, PROMPT, D), 1.0, 6.0, ((0, 8), (1, 2)))
    decode_hidden = gaussian(seeds[1], (PROMPTS, N_REP, 2, SAMP * STEPS, D), 1.0, 6.0, ((0, 8), (1, 2)))
    norm_gain = jnp.clip(1.0 + 0.15 * jax.random.normal(seeds[2], (D,), jnp.float32), 0.25, 1.75).astype(jnp.bfloat16)
    qkv_weight = gaussian(seeds[3], (D, KVH * (QPK + 2) * HD), D ** -0.5, 0.0625, ((0, 8), (1, 2)))
    qkv_bias = draw_qkv_bias(jax.random.fold_in(seeds[6], 71), 0)
    lengths = draw_lengths(jax.random.fold_in(seeds[6], 71), 0)
    return dict(hidden=hidden, decode_hidden=decode_hidden, norm_gain=norm_gain, qkv_weight=qkv_weight, qkv_bias=qkv_bias, lengths=lengths)


THETA = 1000000.0
EPSILON = 1e-06
NEGATIVE = -1e+30

def normalize(row_block, gain_row):
    widened = row_block.astype(jnp.float32)
    factor = lax.rsqrt(lax.optimization_barrier(jnp.mean(widened * widened, axis=-1, keepdims=True)) + EPSILON)
    return (widened * factor * gain_row.astype(jnp.float32)).astype(jnp.bfloat16)

def rope_tables(positions):
    half_size = HD // 2
    frequency = THETA ** (-(jnp.arange(half_size, dtype=jnp.float32) * 2.0 / HD))
    angle = positions.astype(jnp.float32)[:, None] * frequency[None, :]
    return (jnp.cos(angle), jnp.sin(angle))

def rotate(vector, cosine, sine_part):
    half_size = vector.shape[-1] // 2
    first_half = vector[..., :half_size]
    second = vector[..., half_size:]
    return jnp.concatenate([first_half * cosine - second * sine_part, second * cosine + first_half * sine_part], axis=-1)

def qkv_rows(row_block, positions, norm_gain, qkv_weight, qkv_bias):
    normed = normalize(row_block, norm_gain)
    projected = jnp.dot(normed, qkv_weight, preferred_element_type=jnp.float32) + qkv_bias.astype(jnp.float32)
    projected = projected.reshape(row_block.shape[0], KVH, QPK + 2, HD)
    cosine, sine_part = rope_tables(positions)
    query_matrix = rotate(projected[:, :, :QPK], cosine[:, None, None, :], sine_part[:, None, None, :]).astype(jnp.bfloat16)
    key_matrix_rows = rotate(projected[:, :, QPK], cosine[:, None, :], sine_part[:, None, :]).astype(jnp.bfloat16)
    value_matrix = projected[:, :, QPK + 1].astype(jnp.bfloat16)
    return (query_matrix, key_matrix_rows, value_matrix)

def attend(head_query, head_keys, per_head_value_rows, allowed):
    scores = jnp.einsum('nqd,md->qnm', head_query.astype(jnp.float32), head_keys.astype(jnp.float32)) * HD ** (-0.5)
    highest = lax.optimization_barrier(jnp.max(jnp.where(allowed[None], scores, NEGATIVE), axis=-1, keepdims=True))
    exponent = jnp.where(allowed[None], jnp.exp(scores - highest), 0.0)
    running = lax.optimization_barrier(jnp.sum(exponent, axis=-1, keepdims=True))
    weight_matrix = (exponent / running).astype(jnp.bfloat16)
    return jnp.einsum('qnm,md->nqd', weight_matrix.astype(jnp.float32), per_head_value_rows.astype(jnp.float32))

def heads_attend(query_matrix, key_matrix_rows, value_matrix, allowed):

    def single_head(item_tuple):
        head_query, head_keys, per_head_value_rows = item_tuple
        return attend(head_query, head_keys, per_head_value_rows, allowed)
    result = lax.map(single_head, (jnp.swapaxes(query_matrix, 0, 1), jnp.swapaxes(key_matrix_rows, 0, 1), jnp.swapaxes(value_matrix, 0, 1)))
    return jnp.swapaxes(result, 0, 1)

def reference(hidden, decode_hidden, norm_gain, qkv_weight, qkv_bias, lengths):

    def prefill_one(item_tuple):
        row_block, valid_len = item_tuple
        positions = jnp.arange(PROMPT, dtype=jnp.int32)
        query_matrix, key_matrix_rows, value_matrix = qkv_rows(row_block, positions, norm_gain, qkv_weight, qkv_bias)
        allowed = (positions[None, :] <= positions[:, None]) & (positions[None, :] < valid_len)
        result = heads_attend(query_matrix, key_matrix_rows, value_matrix, allowed)
        return (result.astype(jnp.bfloat16).reshape(PROMPT, KVH * QPK * HD), key_matrix_rows, value_matrix)
    prefill_out, keys_all, values_all = lax.map(prefill_one, (hidden, lengths))

    def decode_group(row_block, prompt_keys, prompt_values, valid_len):
        row_ids = jnp.arange(SAMP * STEPS, dtype=jnp.int32)
        step_ids = row_ids % STEPS
        sample_ids = row_ids // STEPS
        positions = valid_len + step_ids
        query_matrix, key_matrix_rows, value_matrix = qkv_rows(row_block, positions, norm_gain, qkv_weight, qkv_bias)
        all_keys = jnp.concatenate([prompt_keys, key_matrix_rows], axis=0)
        all_values = jnp.concatenate([prompt_values, value_matrix], axis=0)
        prompt_allowed = jnp.broadcast_to((jnp.arange(PROMPT, dtype=jnp.int32) < valid_len)[None, :], (SAMP * STEPS, PROMPT))
        own_allowed = (sample_ids[None, :] == sample_ids[:, None]) & (step_ids[None, :] <= step_ids[:, None])
        allowed = jnp.concatenate([prompt_allowed, own_allowed], axis=1)
        result = heads_attend(query_matrix, all_keys, all_values, allowed)
        return result.astype(jnp.bfloat16).reshape(SAMP * STEPS, KVH * QPK * HD)

    def decode_one(item_tuple):
        grp_index, rows_all = item_tuple
        results = []
        for rep_index in range(N_REP):
            pair_list = []
            for side_index in range(2):
                prompt = (grp_index + side_index * (PROMPTS // 2)) % PROMPTS
                pair_list.append(decode_group(rows_all[rep_index, side_index], keys_all[prompt], values_all[prompt], lengths[prompt]))
            results.append(jnp.stack(pair_list))
        return jnp.stack(results)
    decode_out = lax.map(decode_one, (jnp.arange(PROMPTS, dtype=jnp.int32), decode_hidden))
    return (prefill_out, decode_out)
```

```python
import jax
import jax.numpy as jnp
from jax import lax
from jax.experimental import pallas as pl
from jax.experimental.pallas import tpu as pltpu
from jax.sharding import PartitionSpec as P
import functools
import math

HD = 128
QPK = 8
STEPS = 4


THETA = 1000000.0
EPSILON = 1e-06
NEGATIVE = -1e30


def shifted(block, axis, distance):
    devices = range(lax.axis_size(axis))
    route = [((i - distance) % len(devices), i) for i in devices]
    return lax.ppermute(block, axis, route)


def normalize(row_block, gain_row):
    widened = row_block.astype(jnp.float32)
    factor = lax.rsqrt(jnp.mean(widened * widened, axis=-1, keepdims=True) + EPSILON)
    return (widened * factor * gain_row.astype(jnp.float32)).astype(jnp.bfloat16)


def rope_tables(positions, head_size):
    half_size = head_size // 2
    frequency = THETA ** (-(jnp.arange(half_size, dtype=jnp.float32) * 2.0 / head_size))
    angle = positions.astype(jnp.float32)[:, None] * frequency[None, :]
    return (jnp.cos(angle), jnp.sin(angle))


def rotate(vector, cosine, sine_part):
    half_size = vector.shape[-1] // 2
    first_half = vector[..., :half_size]
    second = vector[..., half_size:]
    return jnp.concatenate(
        [first_half * cosine - second * sine_part, second * cosine + first_half * sine_part],
        axis=-1,
    )


def masked_max(scores, allowed):
    return jnp.max(jnp.where(allowed, scores, NEGATIVE), axis=-1, keepdims=True)


def combine_values(weight_matrix, value_matrix):
    return jnp.einsum(
        "aprk,kaz->rapz",
        weight_matrix.astype(jnp.bfloat16),
        value_matrix,
        preferred_element_type=jnp.float32,
    )


def pair_scores(query_matrix, key_matrix_rows, score_scale):
    return (
        jnp.einsum(
            "wjro,ujo->jrwu", query_matrix, key_matrix_rows, preferred_element_type=jnp.float32
        )
        * score_scale
    )


def decode_pair(
    query_matrix,
    own_keys,
    own_values,
    prompt_keys,
    prompt_values,
    valid_len,
    local_allowed,
    score_scale,
):
    key_slot_index = jnp.arange(prompt_keys.shape[0], dtype=jnp.int32)
    prompt_allowed = (key_slot_index < valid_len)[None, None, None, :]
    far_scores = pair_scores(query_matrix, prompt_keys, score_scale)
    near_scores = pair_scores(query_matrix, own_keys, score_scale)
    highest = jnp.maximum(
        masked_max(far_scores, prompt_allowed), masked_max(near_scores, local_allowed)
    )
    far_exp = jnp.where(prompt_allowed, jnp.exp(far_scores - highest), 0.0)
    near_exp = jnp.where(local_allowed, jnp.exp(near_scores - highest), 0.0)
    running = jnp.sum(far_exp, axis=-1, keepdims=True) + jnp.sum(near_exp, axis=-1, keepdims=True)
    return combine_values(far_exp / running, prompt_values) + combine_values(
        near_exp / running, own_values
    )


def plain_device(hidden, decode_hidden, norm_gain, qkv_weight, qkv_bias, lengths):
    prompt_count = lax.axis_size("grp")
    rep_count = lax.axis_size("rep")
    half_cycle = prompt_count // 2
    grp_here = lax.axis_index("grp")
    rep_here = lax.axis_index("rep")
    span_rows = hidden.shape[1]
    model_width = hidden.shape[2]
    head_block = (QPK + 2) * HD
    heads_here = qkv_bias.shape[0] // head_block
    decode_rows = decode_hidden.shape[3]
    score_scale = HD ** (-0.5)
    prefill_normed = normalize(hidden[0], norm_gain)
    decode_normed = normalize(decode_hidden.reshape(2 * decode_rows, model_width), norm_gain)
    normed = jnp.concatenate([prefill_normed, decode_normed], axis=0)
    share_cols = qkv_weight.shape[1] // rep_count
    own_cols = lax.dynamic_slice_in_dim(qkv_weight, rep_here * share_cols, share_cols, 1)
    columns = lax.all_gather(own_cols, "grp", axis=0, tiled=True)
    complete = lax.all_gather(columns, "rep", axis=1, tiled=True)
    projected = jnp.dot(normed, complete, preferred_element_type=jnp.float32)
    projected = (projected + qkv_bias.astype(jnp.float32)).reshape(
        normed.shape[0], heads_here, QPK + 2, HD
    )
    index_table = jnp.arange(prompt_count, dtype=jnp.int32)

    def length_of(prompt):
        return jnp.sum(jnp.where(index_table == prompt, lengths, 0))

    own_len = length_of(grp_here)
    far_len = length_of((grp_here + half_cycle) % prompt_count)
    row_position = rep_here * span_rows + jnp.arange(span_rows, dtype=jnp.int32)
    local_ids = jnp.arange(decode_rows, dtype=jnp.int32)
    step_ids = local_ids % STEPS
    sample_ids = local_ids // STEPS
    positions = jnp.concatenate([row_position, own_len + step_ids, far_len + step_ids])
    cosine, sine_part = rope_tables(positions, HD)
    query_matrix = rotate(
        projected[:, :, :QPK], cosine[:, None, None, :], sine_part[:, None, None, :]
    ).astype(jnp.bfloat16)
    key_matrix_rows = rotate(
        projected[:, :, QPK], cosine[:, None, :], sine_part[:, None, :]
    ).astype(jnp.bfloat16)
    value_matrix = projected[:, :, QPK + 1].astype(jnp.bfloat16)
    cache_keys, cache_values = (
        lax.all_gather(key_matrix_rows[:span_rows], "rep", axis=0, tiled=True),
        lax.all_gather(value_matrix[:span_rows], "rep", axis=0, tiled=True),
    )
    key_pos = jnp.arange(cache_keys.shape[0], dtype=jnp.int32)
    allowed = ((key_pos[None, :] <= row_position[:, None]) & (key_pos[None, :] < own_len))[
        None, None
    ]
    scores = pair_scores(query_matrix[:span_rows], cache_keys, score_scale)
    highest = masked_max(scores, allowed)
    exponent = jnp.where(allowed, jnp.exp(scores - highest), 0.0)
    weight_matrix = exponent / jnp.sum(exponent, axis=-1, keepdims=True)
    attended = combine_values(weight_matrix, cache_values)
    prefill_out = attended.astype(jnp.bfloat16).reshape(1, span_rows, heads_here * QPK * HD)
    decode_queries = query_matrix[span_rows:].reshape(2, decode_rows, heads_here, QPK, HD)
    decode_keys = key_matrix_rows[span_rows:].reshape(2, decode_rows, heads_here, HD)
    decode_values = value_matrix[span_rows:].reshape(2, decode_rows, heads_here, HD)
    local_allowed = (
        (sample_ids[None, :] == sample_ids[:, None]) & (step_ids[None, :] <= step_ids[:, None])
    )[None, None]
    near_out = decode_pair(
        decode_queries[0],
        decode_keys[0],
        decode_values[0],
        cache_keys,
        cache_values,
        own_len,
        local_allowed,
        score_scale,
    )
    far_keys, far_values = shifted((cache_keys, cache_values), "grp", half_cycle)
    far_out = decode_pair(
        decode_queries[1],
        decode_keys[1],
        decode_values[1],
        far_keys,
        far_values,
        far_len,
        local_allowed,
        score_scale,
    )
    decode_out = (
        jnp.stack([near_out, far_out])
        .astype(jnp.bfloat16)
        .reshape(1, 1, 2, decode_rows, heads_here * QPK * HD)
    )
    return (prefill_out, decode_out)


TILE = 512
MESH = pl.DeviceIdType.MESH


def gather_kernel(
    size, rows_up, hidden_ref, decode_ref, gain_ref, w_ref,
    acc_ref, wa_ref, wb_ref,
    x_ref, wt_ref, sa, ra, sb, rb, sx, rx, lx, lt,
):
    count = size
    depth = count // 2
    g = lax.axis_index("grp")
    r = lax.axis_index("rep")
    z = g // 2
    y = g % 2
    half = count // 2
    far = (g + half) % count
    span = hidden_ref.shape[1]
    drows = decode_ref.shape[3]
    share = w_ref.shape[0]
    cols_a = wa_ref.shape[2]
    cols_b = wb_ref.shape[2]
    tiles_a = cols_a // TILE
    tiles_b = cols_b // TILE
    base = pl.multiple_of(r * (cols_a + cols_b), 128)
    base_b = pl.multiple_of(r * (cols_a + cols_b) + cols_a, 128)

    barrier = pltpu.get_barrier_semaphore()

    def greet(grp, rep):
        pl.semaphore_signal(barrier, inc=1, device_id={"grp": grp, "rep": rep}, device_id_type=MESH)

    greet(z * 2 + 1 - y, r)
    greet(g, 1 - r)
    greet(far, r)

    @pl.when(z >= 1)
    def _():
        greet(g - 2, r)

    @pl.when(z + 1 < depth)
    def _():
        greet(g + 2, r)

    inner = (z >= 1) & (z + 1 < depth)

    @pl.when(inner)
    def _():
        pl.semaphore_wait(barrier, 5)

    @pl.when(jnp.logical_not(inner))
    def _():
        pl.semaphore_wait(barrier, 4)

    def way(direction):
        return (g - 2, g + 2, z * 2 + 1 - y)[direction]

    def copy_a(o, direction, own):
        src = w_ref.at[:, pl.ds(base, cols_a)] if own else wa_ref.at[o]
        return pltpu.make_async_remote_copy(
            src, wa_ref.at[o], sa.at[o, direction], ra.at[o],
            device_id={"grp": way(direction)}, device_id_type=MESH,
        )

    def copy_b(o, direction, own):
        src = w_ref.at[:, pl.ds(base_b, cols_b)] if own else wb_ref.at[o]
        return pltpu.make_async_remote_copy(
            src, wb_ref.at[o], sb.at[o, direction], rb.at[o],
            device_id={"grp": way(direction)}, device_id_type=MESH,
        )

    def along(make, o, own, left, right):
        @pl.when(left)
        def _():
            make(o, 0, own).start()

        @pl.when(right)
        def _():
            make(o, 1, own).start()

    row_h = pl.multiple_of(r * span, 16)
    row_n = pl.multiple_of(2 * span + r * drows, 16)
    row_f = pl.multiple_of(2 * span + (2 + r) * drows, 16)
    row_o = pl.multiple_of(2 * span + (3 - r) * drows, 16)
    sib = {"rep": 1 - r}

    def send(src, row, n, i, device):
        return pltpu.make_async_remote_copy(
            src, x_ref.at[pl.ds(row, n), :], sx.at[i], rx.at[i], device_id=device, device_id_type=MESH
        )

    far_send = send(decode_ref.at[0, 0, 1], row_f, drows, 0, {"grp": far})
    far_send.start()
    along(copy_a, g, True, z >= 1, z + 1 < depth)
    copy_b(g, 2, True).start()
    copy_a(g, 2, True).start()
    hid_send = send(hidden_ref.at[0], row_h, span, 1, sib)
    near_send = send(decode_ref.at[0, 0, 0], row_n, drows, 2, sib)
    hid_send.start()
    near_send.start()
    own_h = pltpu.make_async_copy(hidden_ref.at[0], x_ref.at[pl.ds(row_h, span), :], lx.at[0])
    own_n = pltpu.make_async_copy(decode_ref.at[0, 0, 0], x_ref.at[pl.ds(row_n, drows), :], lx.at[1])
    own_h.start()
    own_n.start()

    @pl.loop(0, acc_ref.shape[0] // 16)
    def _(i):
        acc_ref[pl.ds(pl.multiple_of(i * 16, 16), 16), :] = jnp.zeros((16, acc_ref.shape[1]), jnp.float32)

    own_h.wait()
    own_n.wait()
    far_send.wait_recv()
    forward = send(x_ref.at[pl.ds(row_f, drows), :], row_f, drows, 3, sib)
    forward.start()
    hid_send.wait_recv()
    near_send.wait_recv()
    send(x_ref.at[pl.ds(row_o, drows), :], row_o, drows, 3, sib).wait_recv()
    forward.wait_send()
    gain = gain_ref[...].astype(jnp.float32)

    @pl.loop(0, x_ref.shape[0] // 16)
    def _(i):
        rows = pl.ds(pl.multiple_of(i * 16, 16), 16)
        wide = x_ref[rows, :].astype(jnp.float32)
        factor = lax.rsqrt(jnp.mean(wide * wide, axis=-1, keepdims=True) + EPSILON)
        x_ref[rows, :] = (wide * factor * gain).astype(jnp.bfloat16)

    def multiply(o, tiles, first, land_ref, own_base):
        def fetch(t, slot):
            off = pl.multiple_of(t * TILE, 128)

            @pl.when(o == g)
            def _():
                pltpu.make_async_copy(
                    w_ref.at[:, pl.ds(pl.multiple_of(own_base + off, 128), TILE)], wt_ref.at[slot], lt.at[slot]
                ).start()

            @pl.when(o != g)
            def _():
                pltpu.make_async_copy(
                    land_ref.at[o, :, pl.ds(off, TILE)], wt_ref.at[slot], lt.at[slot]
                ).start()

        fetch(0, 0)

        @pl.loop(0, tiles)
        def _(t):
            slot = t % 2

            @pl.when(t + 1 < tiles)
            def _():
                fetch(t + 1, (t + 1) % 2)

            pltpu.make_async_copy(land_ref.at[0, :, pl.ds(0, TILE)], wt_ref.at[slot], lt.at[slot]).wait()
            cols = pl.ds(pl.multiple_of(first + t * TILE, 128), TILE)
            acc_ref[:, cols] += jnp.dot(
                x_ref[:, pl.ds(pl.multiple_of(o * share, 128), share)], wt_ref[slot],
                preferred_element_type=jnp.float32,
            )

    def arrive_b(k):
        for sign in (-1, 1):
            zz = z + sign * k

            @pl.when((zz >= 0) & (zz < depth))
            def _():
                for yy in (0, 1):
                    o = zz * 2 + yy
                    copy_b(o, 2, False).wait_recv()
                    if sign < 0:
                        along(copy_b, o, False, z < 0, z + 1 < depth)
                    else:
                        along(copy_b, o, False, z >= 1, z < 0)

    def multiply_b(low, high):
        @pl.loop(0, count)
        def _(o):
            hop = o // 2 - z

            @pl.when(((hop >= low) & (hop <= high)) | ((-hop >= low) & (-hop <= high)))
            def _():
                multiply(o, tiles_b, cols_a, wb_ref, base_b)

    issue = max(1, depth - 2)

    @pl.loop(0, 4 * (depth + 1))
    def _(e):
        k = e // 4
        s = e % 4
        side = s // 2
        right = s % 2
        kk = k - side
        zz = z + (2 * right - 1) * kk
        yy = (y + side) % 2
        o = zz * 2 + yy

        @pl.when((k == issue) & (s == 2))
        def _():
            partner = z * 2 + 1 - y
            copy_b(partner, 2, False).wait_recv()
            along(copy_b, g, True, z >= 1, z + 1 < depth)
            along(copy_b, partner, False, z >= 1, z + 1 < depth)

        @pl.when((k == depth - 1) & (s == 2))
        def _():
            for hop in range(1, depth - 1):
                arrive_b(hop)

        @pl.when((k == depth) & (s == 0))
        def _():
            multiply_b(0, depth - 2)

        @pl.when((kk >= 0) & (zz >= 0) & (zz < depth) & ((kk > 0) | (right == 0)))
        def _():
            @pl.when(o != g)
            def _():
                copy_a(o, 2, False).wait_recv()

            @pl.when((side == 0) & (kk > 0))
            def _():
                along(copy_a, o, False, (right == 1) & (z >= 1), (right == 0) & (z + 1 < depth))
                copy_a(o, 2, False).start()

            multiply(o, tiles_a, 0, wa_ref, base)

    arrive_b(depth - 1)
    multiply_b(depth - 1, depth - 1)

    far_send.wait_send()
    hid_send.wait_send()
    near_send.wait_send()

    @pl.loop(0, count)
    def _(o):
        zo = o // 2
        to_left = (zo >= z) & (z >= 1)
        to_right = (zo <= z) & (z + 1 < depth)

        @pl.when(o % 2 == y)
        def _():
            @pl.when(to_left)
            def _():
                copy_a(o, 0, False).wait_send()

            @pl.when(to_right)
            def _():
                copy_a(o, 1, False).wait_send()

            copy_a(o, 2, False).wait_send()

        @pl.when(to_left)
        def _():
            copy_b(o, 0, False).wait_send()

        @pl.when(to_right)
        def _():
            copy_b(o, 1, False).wait_send()

    copy_b(g, 2, False).wait_send()


def gather_project(hidden, decode_hidden, norm_gain, qkv_weight, reps):
    count = lax.axis_size("grp")
    rows = reps * (hidden.shape[1] + 2 * decode_hidden.shape[3])
    share = qkv_weight.shape[0]
    width = hidden.shape[2]
    cols = qkv_weight.shape[1] // reps
    tiles = cols // TILE
    cols_b = max(1, tiles // 5) * TILE
    cols_a = cols - cols_b
    hbm = pl.BlockSpec(memory_space=pl.ANY)
    vmem = pl.BlockSpec(memory_space=pltpu.VMEM)
    dma = pltpu.SemaphoreType.DMA
    return pl.pallas_call(
        functools.partial(gather_kernel, count, rows),
        out_shape=(
            jax.ShapeDtypeStruct((rows, cols), jnp.float32),
            jax.ShapeDtypeStruct((count, share, cols_a), jnp.bfloat16),
            jax.ShapeDtypeStruct((count, share, cols_b), jnp.bfloat16),
        ),
        in_specs=[hbm, hbm, vmem, hbm],
        out_specs=(vmem, hbm, hbm),
        scratch_shapes=[
            pltpu.VMEM((rows, width), jnp.bfloat16),
            pltpu.VMEM((2, share, TILE), jnp.bfloat16),
            dma((count, 3)), dma((count,)),
            dma((count, 3)), dma((count,)),
            dma((4,)), dma((4,)), dma((2,)), dma((2,)),
        ],
        compiler_params=pltpu.CompilerParams(
            collective_id=0, has_side_effects=True, vmem_limit_bytes=56 << 20
        ),
        name="gather_project",
    )(hidden, decode_hidden, norm_gain.reshape(1, width), qkv_weight)[0]


def attend_kernel(prompt_rows, block, len_ref, proj_ref, bias_ref, cos_ref, sin_ref, out_ref, q_ref, k_ref, v_ref, m_ref):
    rows = proj_ref.shape[0]
    cosine = cos_ref[...]
    sine = sin_ref[...]
    factor = HD ** (-0.5) * math.log2(math.e)
    valid = len_ref[0]

    def part(j):
        cols = slice(j * HD, (j + 1) * HD)
        return proj_ref[:, cols] + bias_ref[:, cols]

    def turned(x):
        return x * cosine + pltpu.roll(x, HD // 2, 1) * sine

    for j in range(QPK):
        q_ref[j] = (turned(part(j)) * factor).astype(jnp.bfloat16)
    k_ref[...] = turned(part(QPK)).astype(jnp.bfloat16)
    v_ref[...] = part(QPK + 1).astype(jnp.bfloat16)

    def run(start, size, keys):
        shape = (size, keys)
        row = lax.broadcasted_iota(jnp.int32, shape, 0) + start
        col = lax.broadcasted_iota(jnp.int32, shape, 1)
        if start < prompt_rows:
            allowed = (col <= row) & (col < valid)
        else:
            same = ((row - prompt_rows) // STEPS == (col - prompt_rows) // STEPS) & (col <= row)
            allowed = (col < jnp.minimum(valid, prompt_rows)) | ((col >= prompt_rows) & same)
        m_ref[:size, :keys] = jnp.where(allowed, 0.0, NEGATIVE)

        for j in range(QPK):
            s = lax.dot_general(
                q_ref[j, start:start + size, :], k_ref[:keys, :], (((1,), (1,)), ((), ())),
                preferred_element_type=jnp.float32,
            ) + m_ref[:size, :keys]
            top = jnp.max(s, axis=-1, keepdims=True)
            p = jnp.exp2(s - top)
            total = jnp.sum(p, axis=-1, keepdims=True)
            o = jnp.dot(p.astype(jnp.bfloat16), v_ref[:keys, :], preferred_element_type=jnp.float32)
            out_ref[start:start + size, j * HD:(j + 1) * HD] = (o / total).astype(jnp.bfloat16)

    for start in range(0, prompt_rows, block):
        run(start, block, start + block)
    run(prompt_rows, rows - prompt_rows, rows)


def attend(proj, bias_row, cosine, sine, valid, prompt_rows):
    rows, cols = proj.shape
    head = (QPK + 2) * HD
    heads = cols // head
    block = 256 if prompt_rows % 256 == 0 else prompt_rows
    size = max(block, rows - prompt_rows)
    return pl.pallas_call(
        functools.partial(attend_kernel, prompt_rows, block),
        out_shape=jax.ShapeDtypeStruct((rows, heads * QPK * HD), jnp.bfloat16),
        grid=(heads,),
        in_specs=[
            pl.BlockSpec(memory_space=pltpu.SMEM),
            pl.BlockSpec((rows, head), lambda h: (0, h)),
            pl.BlockSpec((1, head), lambda h: (0, h)),
            pl.BlockSpec((rows, HD), lambda h: (0, 0)),
            pl.BlockSpec((rows, HD), lambda h: (0, 0)),
        ],
        out_specs=pl.BlockSpec((rows, QPK * HD), lambda h: (0, h)),
        scratch_shapes=[
            pltpu.VMEM((QPK, rows, HD), jnp.bfloat16),
            pltpu.VMEM((rows, HD), jnp.bfloat16),
            pltpu.VMEM((rows, HD), jnp.bfloat16),
            pltpu.VMEM((size, rows), jnp.float32),
        ],
        compiler_params=pltpu.CompilerParams(vmem_limit_bytes=48 << 20),
        name="attend",
    )(valid.reshape(1), proj, bias_row, cosine, sine)


def on_device(hidden, decode_hidden, norm_gain, qkv_weight, qkv_bias, lengths):
    count = lax.axis_size("grp")
    reps = lax.axis_size("rep")
    head_block = (QPK + 2) * HD
    heads_here = qkv_bias.shape[0] // head_block
    cols = qkv_weight.shape[1] // reps
    if reps != 2 or count % 2 or count < 4 or heads_here % reps or cols % TILE or cols < 2 * TILE:
        return plain_device(hidden, decode_hidden, norm_gain, qkv_weight, qkv_bias, lengths)
    g = lax.axis_index("grp")
    r = lax.axis_index("rep")
    half = count // 2
    span = hidden.shape[1]
    drows = decode_hidden.shape[3]
    prompt_rows = reps * span
    proj = gather_project(hidden, decode_hidden, norm_gain, qkv_weight, reps)

    index_table = jnp.arange(count, dtype=jnp.int32)
    own_len = jnp.sum(jnp.where(index_table == g, lengths, 0))
    steps = jnp.arange(2 * reps * drows, dtype=jnp.int32) % STEPS
    positions = jnp.concatenate([jnp.arange(prompt_rows, dtype=jnp.int32), own_len + steps])
    cosine, sine = rope_tables(positions, HD)
    cosine = jnp.concatenate([cosine, cosine], axis=-1)
    sine = jnp.concatenate([-sine, sine], axis=-1)
    bias_row = lax.dynamic_slice_in_dim(qkv_bias, r * cols, cols, 0).astype(jnp.float32).reshape(1, cols)
    out = attend(proj, bias_row, cosine, sine, own_len, prompt_rows)
    width = out.shape[1]

    def pick(block, which):
        return lax.dynamic_index_in_dim(block, which, 0, keepdims=False)

    swap = [(0, 1), (1, 0)]
    main = out[:prompt_rows].reshape(reps, span, width)
    near = out[prompt_rows:prompt_rows + 2 * drows].reshape(reps, drows, width)
    far = out[prompt_rows + 2 * drows:].reshape(reps, drows, width)
    other_main = lax.ppermute(pick(main, 1 - r), "rep", swap)
    other_near = lax.ppermute(pick(near, 1 - r), "rep", swap)
    far_same = lax.ppermute(pick(far, r), "grp", [(p, (p - half) % count) for p in range(count)])
    cross = [
        (p * reps + c, ((p - half) % count) * reps + 1 - c) for p in range(count) for c in range(reps)
    ]
    far_other = lax.ppermute(pick(far, 1 - r), ("grp", "rep"), cross)

    def join(mine, other):
        return jnp.where(
            r == 0, jnp.concatenate([mine, other], axis=-1), jnp.concatenate([other, mine], axis=-1)
        )

    prefill_out = join(pick(main, r), other_main)[None]
    decode_out = jnp.stack([join(pick(near, r), other_near), join(far_same, far_other)])[None, None]
    return (prefill_out, decode_out)


def solution(mesh):
    return jax.shard_map(
        on_device,
        mesh=mesh,
        in_specs=(
            P("grp", "rep", None),
            P("grp", "rep", None, None, None),
            P(),
            P("grp", "tp"),
            P("tp"),
            P(),
        ),
        out_specs=(P("grp", "rep", "tp"), P("grp", "rep", None, None, "tp")),
        check_vma=False,
    )
```

```python
import jax
import jax.numpy as jnp
from jax import lax
from jax.experimental import pallas as pl
from jax.experimental.pallas import tpu as pltpu
from jax.sharding import PartitionSpec as P
import functools
import math

HD = 128
QPK = 8
STEPS = 4


THETA = 1000000.0
EPSILON = 1e-06
NEGATIVE = -1e30


def shifted(block, axis, distance):
    devices = range(lax.axis_size(axis))
    route = [((i - distance) % len(devices), i) for i in devices]
    return lax.ppermute(block, axis, route)


def normalize(row_block, gain_row):
    widened = row_block.astype(jnp.float32)
    factor = lax.rsqrt(jnp.mean(widened * widened, axis=-1, keepdims=True) + EPSILON)
    return (widened * factor * gain_row.astype(jnp.float32)).astype(jnp.bfloat16)


def rope_tables(positions, head_size):
    half_size = head_size // 2
    frequency = THETA ** (-(jnp.arange(half_size, dtype=jnp.float32) * 2.0 / head_size))
    angle = positions.astype(jnp.float32)[:, None] * frequency[None, :]
    return (jnp.cos(angle), jnp.sin(angle))


def rotate(vector, cosine, sine_part):
    half_size = vector.shape[-1] // 2
    first_half = vector[..., :half_size]
    second = vector[..., half_size:]
    return jnp.concatenate(
        [first_half * cosine - second * sine_part, second * cosine + first_half * sine_part],
        axis=-1,
    )


def masked_max(scores, allowed):
    return jnp.max(jnp.where(allowed, scores, NEGATIVE), axis=-1, keepdims=True)


def combine_values(weight_matrix, value_matrix):
    return jnp.einsum(
        "aprk,kaz->rapz",
        weight_matrix.astype(jnp.bfloat16),
        value_matrix,
        preferred_element_type=jnp.float32,
    )


def pair_scores(query_matrix, key_matrix_rows, score_scale):
    return (
        jnp.einsum(
            "wjro,ujo->jrwu", query_matrix, key_matrix_rows, preferred_element_type=jnp.float32
        )
        * score_scale
    )


def decode_pair(
    query_matrix,
    own_keys,
    own_values,
    prompt_keys,
    prompt_values,
    valid_len,
    local_allowed,
    score_scale,
):
    key_slot_index = jnp.arange(prompt_keys.shape[0], dtype=jnp.int32)
    prompt_allowed = (key_slot_index < valid_len)[None, None, None, :]
    far_scores = pair_scores(query_matrix, prompt_keys, score_scale)
    near_scores = pair_scores(query_matrix, own_keys, score_scale)
    highest = jnp.maximum(
        masked_max(far_scores, prompt_allowed), masked_max(near_scores, local_allowed)
    )
    far_exp = jnp.where(prompt_allowed, jnp.exp(far_scores - highest), 0.0)
    near_exp = jnp.where(local_allowed, jnp.exp(near_scores - highest), 0.0)
    running = jnp.sum(far_exp, axis=-1, keepdims=True) + jnp.sum(near_exp, axis=-1, keepdims=True)
    return combine_values(far_exp / running, prompt_values) + combine_values(
        near_exp / running, own_values
    )


def plain_device(hidden, decode_hidden, norm_gain, qkv_weight, qkv_bias, lengths):
    prompt_count = lax.axis_size("grp")
    rep_count = lax.axis_size("rep")
    half_cycle = prompt_count // 2
    grp_here = lax.axis_index("grp")
    rep_here = lax.axis_index("rep")
    span_rows = hidden.shape[1]
    model_width = hidden.shape[2]
    head_block = (QPK + 2) * HD
    heads_here = qkv_bias.shape[0] // head_block
    decode_rows = decode_hidden.shape[3]
    score_scale = HD ** (-0.5)
    prefill_normed = normalize(hidden[0], norm_gain)
    decode_normed = normalize(decode_hidden.reshape(2 * decode_rows, model_width), norm_gain)
    normed = jnp.concatenate([prefill_normed, decode_normed], axis=0)
    share_cols = qkv_weight.shape[1] // rep_count
    own_cols = lax.dynamic_slice_in_dim(qkv_weight, rep_here * share_cols, share_cols, 1)
    columns = lax.all_gather(own_cols, "grp", axis=0, tiled=True)
    complete = lax.all_gather(columns, "rep", axis=1, tiled=True)
    projected = jnp.dot(normed, complete, preferred_element_type=jnp.float32)
    projected = (projected + qkv_bias.astype(jnp.float32)).reshape(
        normed.shape[0], heads_here, QPK + 2, HD
    )
    index_table = jnp.arange(prompt_count, dtype=jnp.int32)

    def length_of(prompt):
        return jnp.sum(jnp.where(index_table == prompt, lengths, 0))

    own_len = length_of(grp_here)
    far_len = length_of((grp_here + half_cycle) % prompt_count)
    row_position = rep_here * span_rows + jnp.arange(span_rows, dtype=jnp.int32)
    local_ids = jnp.arange(decode_rows, dtype=jnp.int32)
    step_ids = local_ids % STEPS
    sample_ids = local_ids // STEPS
    positions = jnp.concatenate([row_position, own_len + step_ids, far_len + step_ids])
    cosine, sine_part = rope_tables(positions, HD)
    query_matrix = rotate(
        projected[:, :, :QPK], cosine[:, None, None, :], sine_part[:, None, None, :]
    ).astype(jnp.bfloat16)
    key_matrix_rows = rotate(
        projected[:, :, QPK], cosine[:, None, :], sine_part[:, None, :]
    ).astype(jnp.bfloat16)
    value_matrix = projected[:, :, QPK + 1].astype(jnp.bfloat16)
    cache_keys, cache_values = (
        lax.all_gather(key_matrix_rows[:span_rows], "rep", axis=0, tiled=True),
        lax.all_gather(value_matrix[:span_rows], "rep", axis=0, tiled=True),
    )
    key_pos = jnp.arange(cache_keys.shape[0], dtype=jnp.int32)
    allowed = ((key_pos[None, :] <= row_position[:, None]) & (key_pos[None, :] < own_len))[
        None, None
    ]
    scores = pair_scores(query_matrix[:span_rows], cache_keys, score_scale)
    highest = masked_max(scores, allowed)
    exponent = jnp.where(allowed, jnp.exp(scores - highest), 0.0)
    weight_matrix = exponent / jnp.sum(exponent, axis=-1, keepdims=True)
    attended = combine_values(weight_matrix, cache_values)
    prefill_out = attended.astype(jnp.bfloat16).reshape(1, span_rows, heads_here * QPK * HD)
    decode_queries = query_matrix[span_rows:].reshape(2, decode_rows, heads_here, QPK, HD)
    decode_keys = key_matrix_rows[span_rows:].reshape(2, decode_rows, heads_here, HD)
    decode_values = value_matrix[span_rows:].reshape(2, decode_rows, heads_here, HD)
    local_allowed = (
        (sample_ids[None, :] == sample_ids[:, None]) & (step_ids[None, :] <= step_ids[:, None])
    )[None, None]
    near_out = decode_pair(
        decode_queries[0],
        decode_keys[0],
        decode_values[0],
        cache_keys,
        cache_values,
        own_len,
        local_allowed,
        score_scale,
    )
    far_keys, far_values = shifted((cache_keys, cache_values), "grp", half_cycle)
    far_out = decode_pair(
        decode_queries[1],
        decode_keys[1],
        decode_values[1],
        far_keys,
        far_values,
        far_len,
        local_allowed,
        score_scale,
    )
    decode_out = (
        jnp.stack([near_out, far_out])
        .astype(jnp.bfloat16)
        .reshape(1, 1, 2, decode_rows, heads_here * QPK * HD)
    )
    return (prefill_out, decode_out)


TILE = 512
MESH = pl.DeviceIdType.MESH


def gather_kernel(
    size, rows_up, hidden_ref, decode_ref, gain_ref, w_ref,
    acc_ref, wa_ref, wb_ref,
    x_ref, wt_ref, sa, ra, sb, rb, sx, rx, lx, lt,
):
    count = size
    depth = count // 2
    g = lax.axis_index("grp")
    r = lax.axis_index("rep")
    z = g // 2
    y = g % 2
    half = count // 2
    far = (g + half) % count
    span = hidden_ref.shape[1]
    drows = decode_ref.shape[3]
    share = w_ref.shape[0]
    cols_a = wa_ref.shape[2]
    cols_b = wb_ref.shape[2]
    tiles_a = cols_a // TILE
    rest = cols_a % TILE
    base = pl.multiple_of(r * (cols_a + cols_b), 128)
    base_b = pl.multiple_of(r * (cols_a + cols_b) + cols_a, 128)

    barrier = pltpu.get_barrier_semaphore()

    def greet(grp, rep):
        pl.semaphore_signal(barrier, inc=1, device_id={"grp": grp, "rep": rep}, device_id_type=MESH)

    greet(z * 2 + 1 - y, r)
    greet(g, 1 - r)
    greet(far, r)

    @pl.when(z >= 1)
    def _():
        greet(g - 2, r)

    @pl.when(z + 1 < depth)
    def _():
        greet(g + 2, r)

    inner = (z >= 1) & (z + 1 < depth)

    @pl.when(inner)
    def _():
        pl.semaphore_wait(barrier, 5)

    @pl.when(jnp.logical_not(inner))
    def _():
        pl.semaphore_wait(barrier, 4)

    def way(direction):
        return (g - 2, g + 2, z * 2 + 1 - y)[direction]

    def copy_a(o, direction, own):
        src = w_ref.at[:, pl.ds(base, cols_a)] if own else wa_ref.at[o]
        return pltpu.make_async_remote_copy(
            src, wa_ref.at[o], sa.at[o, direction], ra.at[o],
            device_id={"grp": way(direction)}, device_id_type=MESH,
        )

    def copy_b(o, direction, own):
        src = w_ref.at[:, pl.ds(base_b, cols_b)] if own else wb_ref.at[o]
        return pltpu.make_async_remote_copy(
            src, wb_ref.at[o], sb.at[o, direction], rb.at[o],
            device_id={"grp": way(direction)}, device_id_type=MESH,
        )

    def along(make, o, own, left, right):
        @pl.when(left)
        def _():
            make(o, 0, own).start()

        @pl.when(right)
        def _():
            make(o, 1, own).start()

    row_h = pl.multiple_of(r * span, 16)
    row_n = pl.multiple_of(2 * span + r * drows, 16)
    row_f = pl.multiple_of(2 * span + (2 + r) * drows, 16)
    row_o = pl.multiple_of(2 * span + (3 - r) * drows, 16)
    sib = {"rep": 1 - r}

    def send(src, row, n, i, device):
        return pltpu.make_async_remote_copy(
            src, x_ref.at[pl.ds(row, n), :], sx.at[i], rx.at[i], device_id=device, device_id_type=MESH
        )

    far_send = send(decode_ref.at[0, 0, 1], row_f, drows, 0, {"grp": far})
    far_send.start()
    along(copy_a, g, True, z >= 1, z + 1 < depth)
    copy_b(g, 2, True).start()
    copy_a(g, 2, True).start()
    hid_send = send(hidden_ref.at[0], row_h, span, 1, sib)
    near_send = send(decode_ref.at[0, 0, 0], row_n, drows, 2, sib)
    hid_send.start()
    near_send.start()
    own_h = pltpu.make_async_copy(hidden_ref.at[0], x_ref.at[pl.ds(row_h, span), :], lx.at[0])
    own_n = pltpu.make_async_copy(decode_ref.at[0, 0, 0], x_ref.at[pl.ds(row_n, drows), :], lx.at[1])
    own_h.start()
    own_n.start()

    @pl.loop(0, acc_ref.shape[0] // 16)
    def _(i):
        acc_ref[pl.ds(pl.multiple_of(i * 16, 16), 16), :] = jnp.zeros((16, acc_ref.shape[1]), jnp.float32)

    own_h.wait()
    own_n.wait()
    far_send.wait_recv()
    forward = send(x_ref.at[pl.ds(row_f, drows), :], row_f, drows, 3, sib)
    forward.start()
    hid_send.wait_recv()
    near_send.wait_recv()
    send(x_ref.at[pl.ds(row_o, drows), :], row_o, drows, 3, sib).wait_recv()
    forward.wait_send()
    gain = gain_ref[...].astype(jnp.float32)

    @pl.loop(0, x_ref.shape[0] // 16)
    def _(i):
        rows = pl.ds(pl.multiple_of(i * 16, 16), 16)
        wide = x_ref[rows, :].astype(jnp.float32)
        factor = lax.rsqrt(jnp.mean(wide * wide, axis=-1, keepdims=True) + EPSILON)
        x_ref[rows, :] = (wide * factor * gain).astype(jnp.bfloat16)

    def own_tile(off, n, slot_ref, sem):
        return pltpu.make_async_copy(w_ref.at[:, pl.ds(pl.multiple_of(base + off, 128), n)], slot_ref, sem)

    def add_product(o, slot, first):
        cols = pl.ds(pl.multiple_of(first, 128), TILE)
        acc_ref[:, cols] += jnp.dot(
            x_ref[:, pl.ds(pl.multiple_of(o * share, 128), share)], wt_ref[slot],
            preferred_element_type=jnp.float32,
        )

    def multiply(o):
        def fetch(t, slot):
            off = pl.multiple_of(t * TILE, 128)

            @pl.when(o == g)
            def _():
                own_tile(off, TILE, wt_ref.at[slot], lt.at[slot]).start()

            @pl.when(o != g)
            def _():
                pltpu.make_async_copy(wa_ref.at[o, :, pl.ds(off, TILE)], wt_ref.at[slot], lt.at[slot]).start()

        fetch(0, 0)

        @pl.loop(0, tiles_a)
        def _(t):
            slot = t % 2

            @pl.when(t + 1 < tiles_a)
            def _():
                fetch(t + 1, (t + 1) % 2)

            own_tile(0, TILE, wt_ref.at[slot], lt.at[slot]).wait()
            add_product(o, slot, t * TILE)

    def multiply_last(o):
        first = tiles_a * TILE

        @pl.when(o == g)
        def _():
            own_tile(first, TILE, wt_ref.at[0], lt.at[0]).start()
            own_tile(first, TILE, wt_ref.at[0], lt.at[0]).wait()

        @pl.when(o != g)
        def _():
            pieces = [pltpu.make_async_copy(wb_ref.at[o], wt_ref.at[0, :, pl.ds(rest, cols_b)], lt.at[0])]
            if rest:
                pieces.append(pltpu.make_async_copy(
                    wa_ref.at[o, :, pl.ds(first, rest)], wt_ref.at[0, :, pl.ds(0, rest)], lt.at[1]
                ))
            for piece in pieces:
                piece.start()
            for piece in pieces:
                piece.wait()

        add_product(o, 0, first)

    def arrive_b(k):
        for sign in (-1, 1):
            zz = z + sign * k

            @pl.when((zz >= 0) & (zz < depth))
            def _():
                for yy in (0, 1):
                    o = zz * 2 + yy
                    copy_b(o, 2, False).wait_recv()
                    if sign < 0:
                        along(copy_b, o, False, z < 0, z + 1 < depth)
                    else:
                        along(copy_b, o, False, z >= 1, z < 0)

    def multiply_b(low, high):
        @pl.loop(0, count)
        def _(o):
            hop = o // 2 - z

            @pl.when(((hop >= low) & (hop <= high)) | ((-hop >= low) & (-hop <= high)))
            def _():
                multiply_last(o)

    issue = max(1, depth - 2)

    @pl.loop(0, 4 * (depth + 1))
    def _(e):
        k = e // 4
        s = e % 4
        side = s // 2
        right = s % 2
        kk = k - side
        zz = z + (2 * right - 1) * kk
        yy = (y + side) % 2
        o = zz * 2 + yy

        @pl.when((k == issue) & (s == 2))
        def _():
            partner = z * 2 + 1 - y
            copy_b(partner, 2, False).wait_recv()
            along(copy_b, g, True, z >= 1, z + 1 < depth)
            along(copy_b, partner, False, z >= 1, z + 1 < depth)

        @pl.when((k == depth - 1) & (s == 2))
        def _():
            for hop in range(1, depth - 1):
                arrive_b(hop)

        @pl.when((k == depth) & (s == 0))
        def _():
            multiply_b(0, depth - 2)

        @pl.when((kk >= 0) & (zz >= 0) & (zz < depth) & ((kk > 0) | (right == 0)))
        def _():
            @pl.when(o != g)
            def _():
                copy_a(o, 2, False).wait_recv()

            @pl.when((side == 0) & (kk > 0))
            def _():
                along(copy_a, o, False, (right == 1) & (z >= 1), (right == 0) & (z + 1 < depth))
                copy_a(o, 2, False).start()

            multiply(o)

    arrive_b(depth - 1)
    multiply_b(depth - 1, depth - 1)

    far_send.wait_send()
    hid_send.wait_send()
    near_send.wait_send()

    @pl.loop(0, count)
    def _(o):
        zo = o // 2
        to_left = (zo >= z) & (z >= 1)
        to_right = (zo <= z) & (z + 1 < depth)

        @pl.when(o % 2 == y)
        def _():
            @pl.when(to_left)
            def _():
                copy_a(o, 0, False).wait_send()

            @pl.when(to_right)
            def _():
                copy_a(o, 1, False).wait_send()

            copy_a(o, 2, False).wait_send()

        @pl.when(to_left)
        def _():
            copy_b(o, 0, False).wait_send()

        @pl.when(to_right)
        def _():
            copy_b(o, 1, False).wait_send()

    copy_b(g, 2, False).wait_send()


def gather_project(hidden, decode_hidden, norm_gain, qkv_weight, reps):
    count = lax.axis_size("grp")
    rows = reps * (hidden.shape[1] + 2 * decode_hidden.shape[3])
    share = qkv_weight.shape[0]
    width = hidden.shape[2]
    cols = qkv_weight.shape[1] // reps
    cols_b = min(TILE, max(1, round(cols * 0.15 / 128)) * 128)
    cols_a = cols - cols_b
    hbm = pl.BlockSpec(memory_space=pl.ANY)
    vmem = pl.BlockSpec(memory_space=pltpu.VMEM)
    dma = pltpu.SemaphoreType.DMA
    return pl.pallas_call(
        functools.partial(gather_kernel, count, rows),
        out_shape=(
            jax.ShapeDtypeStruct((rows, cols), jnp.float32),
            jax.ShapeDtypeStruct((count, share, cols_a), jnp.bfloat16),
            jax.ShapeDtypeStruct((count, share, cols_b), jnp.bfloat16),
        ),
        in_specs=[hbm, hbm, vmem, hbm],
        out_specs=(vmem, hbm, hbm),
        scratch_shapes=[
            pltpu.VMEM((rows, width), jnp.bfloat16),
            pltpu.VMEM((2, share, TILE), jnp.bfloat16),
            dma((count, 3)), dma((count,)),
            dma((count, 3)), dma((count,)),
            dma((4,)), dma((4,)), dma((2,)), dma((2,)),
        ],
        compiler_params=pltpu.CompilerParams(
            collective_id=0, has_side_effects=True, vmem_limit_bytes=56 << 20
        ),
        name="gather_project",
    )(hidden, decode_hidden, norm_gain.reshape(1, width), qkv_weight)[0]


def attend_kernel(prompt_rows, block, len_ref, proj_ref, bias_ref, cos_ref, sin_ref, out_ref, q_ref, k_ref, v_ref, m_ref):
    rows = proj_ref.shape[0]
    cosine = cos_ref[...]
    sine = sin_ref[...]
    factor = HD ** (-0.5) * math.log2(math.e)
    valid = len_ref[0]

    def part(j):
        cols = slice(j * HD, (j + 1) * HD)
        return proj_ref[:, cols] + bias_ref[:, cols]

    def turned(x):
        return x * cosine + pltpu.roll(x, HD // 2, 1) * sine

    for j in range(QPK):
        q_ref[j] = (turned(part(j)) * factor).astype(jnp.bfloat16)
    k_ref[...] = turned(part(QPK)).astype(jnp.bfloat16)
    v_ref[...] = part(QPK + 1).astype(jnp.bfloat16)

    def run(start, size, keys):
        shape = (size, keys)
        row = lax.broadcasted_iota(jnp.int32, shape, 0) + start
        col = lax.broadcasted_iota(jnp.int32, shape, 1)
        if start < prompt_rows:
            allowed = (col <= row) & (col < valid)
        else:
            same = ((row - prompt_rows) // STEPS == (col - prompt_rows) // STEPS) & (col <= row)
            allowed = (col < jnp.minimum(valid, prompt_rows)) | ((col >= prompt_rows) & same)
        m_ref[:size, :keys] = jnp.where(allowed, 0.0, NEGATIVE)

        for j in range(QPK):
            s = lax.dot_general(
                q_ref[j, start:start + size, :], k_ref[:keys, :], (((1,), (1,)), ((), ())),
                preferred_element_type=jnp.float32,
            ) + m_ref[:size, :keys]
            top = jnp.max(s, axis=-1, keepdims=True)
            p = jnp.exp2(s - top)
            total = jnp.sum(p, axis=-1, keepdims=True)
            o = jnp.dot(p.astype(jnp.bfloat16), v_ref[:keys, :], preferred_element_type=jnp.float32)
            out_ref[start:start + size, j * HD:(j + 1) * HD] = (o / total).astype(jnp.bfloat16)

    for start in range(0, prompt_rows, block):
        run(start, block, start + block)
    run(prompt_rows, rows - prompt_rows, rows)


def attend(proj, bias_row, cosine, sine, valid, prompt_rows):
    rows, cols = proj.shape
    head = (QPK + 2) * HD
    heads = cols // head
    block = 256 if prompt_rows % 256 == 0 else prompt_rows
    size = max(block, rows - prompt_rows)
    return pl.pallas_call(
        functools.partial(attend_kernel, prompt_rows, block),
        out_shape=jax.ShapeDtypeStruct((rows, heads * QPK * HD), jnp.bfloat16),
        grid=(heads,),
        in_specs=[
            pl.BlockSpec(memory_space=pltpu.SMEM),
            pl.BlockSpec((rows, head), lambda h: (0, h)),
            pl.BlockSpec((1, head), lambda h: (0, h)),
            pl.BlockSpec((rows, HD), lambda h: (0, 0)),
            pl.BlockSpec((rows, HD), lambda h: (0, 0)),
        ],
        out_specs=pl.BlockSpec((rows, QPK * HD), lambda h: (0, h)),
        scratch_shapes=[
            pltpu.VMEM((QPK, rows, HD), jnp.bfloat16),
            pltpu.VMEM((rows, HD), jnp.bfloat16),
            pltpu.VMEM((rows, HD), jnp.bfloat16),
            pltpu.VMEM((size, rows), jnp.float32),
        ],
        compiler_params=pltpu.CompilerParams(vmem_limit_bytes=48 << 20),
        name="attend",
    )(valid.reshape(1), proj, bias_row, cosine, sine)


def exchange_kernel(count, out_ref, prefill_ref, decode_ref, ss, rs, ls):
    g = lax.axis_index("grp")
    r = lax.axis_index("rep")
    far = (g + count // 2) % count
    span = prefill_ref.shape[1]
    drows = decode_ref.shape[3]
    width = out_ref.shape[1]
    cols = pl.ds(pl.multiple_of(r * width, 128), width)
    barrier = pltpu.get_barrier_semaphore()
    for grp, rep in ((g, 1 - r), (far, r), (far, 1 - r)):
        pl.semaphore_signal(barrier, inc=1, device_id={"grp": grp, "rep": rep}, device_id_type=MESH)
    pl.semaphore_wait(barrier, 3)

    def rows(start, n):
        return out_ref.at[pl.ds(pl.multiple_of(start, 16), n), :]

    main = prefill_ref.at[0, :, cols]
    near = decode_ref.at[0, 0, 0, :, cols]
    away = decode_ref.at[0, 0, 1, :, cols]
    near_row = 2 * span
    far_row = near_row + 2 * drows

    def send(src, dst, i, grp, rep):
        return pltpu.make_async_remote_copy(
            src, dst, ss.at[i], rs.at[i], device_id={"grp": grp, "rep": rep}, device_id_type=MESH
        )

    sends = [
        send(rows(far_row + r * drows, drows), away, 0, far, r),
        send(rows(far_row + (1 - r) * drows, drows), away, 1, far, 1 - r),
        send(rows((1 - r) * span, span), main, 2, g, 1 - r),
        send(rows(near_row + (1 - r) * drows, drows), near, 3, g, 1 - r),
    ]
    local = [
        pltpu.make_async_copy(rows(r * span, span), main, ls.at[0]),
        pltpu.make_async_copy(rows(near_row + r * drows, drows), near, ls.at[1]),
    ]
    for copy in sends + local:
        copy.start()
    for copy in sends + local:
        copy.wait()


def exchange(out, hidden, decode_hidden, reps):
    dma = pltpu.SemaphoreType.DMA
    hbm = pl.BlockSpec(memory_space=pl.ANY)
    width = reps * out.shape[1]
    return pl.pallas_call(
        functools.partial(exchange_kernel, lax.axis_size("grp")),
        out_shape=(
            jax.ShapeDtypeStruct(hidden.shape[:2] + (width,), jnp.bfloat16),
            jax.ShapeDtypeStruct(decode_hidden.shape[:4] + (width,), jnp.bfloat16),
        ),
        in_specs=[pl.BlockSpec(memory_space=pltpu.VMEM)],
        out_specs=(hbm, hbm),
        scratch_shapes=[dma((4,)), dma((4,)), dma((2,))],
        compiler_params=pltpu.CompilerParams(
            collective_id=1, has_side_effects=True, vmem_limit_bytes=16 << 20
        ),
        name="exchange",
    )(out)


def on_device(hidden, decode_hidden, norm_gain, qkv_weight, qkv_bias, lengths):
    count = lax.axis_size("grp")
    reps = lax.axis_size("rep")
    head_block = (QPK + 2) * HD
    heads_here = qkv_bias.shape[0] // head_block
    cols = qkv_weight.shape[1] // reps
    if reps != 2 or count % 2 or count < 4 or heads_here % reps or cols % TILE or cols < 2 * TILE or decode_hidden.shape[1] != 1:
        return plain_device(hidden, decode_hidden, norm_gain, qkv_weight, qkv_bias, lengths)
    g = lax.axis_index("grp")
    r = lax.axis_index("rep")
    half = count // 2
    span = hidden.shape[1]
    drows = decode_hidden.shape[3]
    prompt_rows = reps * span
    proj = gather_project(hidden, decode_hidden, norm_gain, qkv_weight, reps)

    index_table = jnp.arange(count, dtype=jnp.int32)
    own_len = jnp.sum(jnp.where(index_table == g, lengths, 0))
    steps = jnp.arange(2 * reps * drows, dtype=jnp.int32) % STEPS
    positions = jnp.concatenate([jnp.arange(prompt_rows, dtype=jnp.int32), own_len + steps])
    cosine, sine = rope_tables(positions, HD)
    cosine = jnp.concatenate([cosine, cosine], axis=-1)
    sine = jnp.concatenate([-sine, sine], axis=-1)
    bias_row = lax.dynamic_slice_in_dim(qkv_bias, r * cols, cols, 0).astype(jnp.float32).reshape(1, cols)
    out = attend(proj, bias_row, cosine, sine, own_len, prompt_rows)
    return exchange(out, hidden, decode_hidden, reps)


def solution(mesh):
    return jax.shard_map(
        on_device,
        mesh=mesh,
        in_specs=(
            P("grp", "rep", None),
            P("grp", "rep", None, None, None),
            P(),
            P("grp", "tp"),
            P("tp"),
            P(),
        ),
        out_specs=(P("grp", "rep", "tp"), P("grp", "rep", None, None, "tp")),
        check_vma=False,
    )
```

```python
import jax
import jax.numpy as jnp
from jax import lax
from jax.experimental import pallas as pl
from jax.experimental.pallas import tpu as pltpu
from jax.sharding import PartitionSpec as P
import functools
import math

HD = 128
QPK = 8
STEPS = 4


THETA = 1000000.0
EPSILON = 1e-06
NEGATIVE = -1e30


def shifted(block, axis, distance):
    devices = range(lax.axis_size(axis))
    route = [((i - distance) % len(devices), i) for i in devices]
    return lax.ppermute(block, axis, route)


def normalize(row_block, gain_row):
    widened = row_block.astype(jnp.float32)
    factor = lax.rsqrt(jnp.mean(widened * widened, axis=-1, keepdims=True) + EPSILON)
    return (widened * factor * gain_row.astype(jnp.float32)).astype(jnp.bfloat16)


def rope_tables(positions, head_size):
    half_size = head_size // 2
    frequency = THETA ** (-(jnp.arange(half_size, dtype=jnp.float32) * 2.0 / head_size))
    angle = positions.astype(jnp.float32)[:, None] * frequency[None, :]
    return (jnp.cos(angle), jnp.sin(angle))


def rotate(vector, cosine, sine_part):
    half_size = vector.shape[-1] // 2
    first_half = vector[..., :half_size]
    second = vector[..., half_size:]
    return jnp.concatenate(
        [first_half * cosine - second * sine_part, second * cosine + first_half * sine_part],
        axis=-1,
    )


def masked_max(scores, allowed):
    return jnp.max(jnp.where(allowed, scores, NEGATIVE), axis=-1, keepdims=True)


def combine_values(weight_matrix, value_matrix):
    return jnp.einsum(
        "aprk,kaz->rapz",
        weight_matrix.astype(jnp.bfloat16),
        value_matrix,
        preferred_element_type=jnp.float32,
    )


def pair_scores(query_matrix, key_matrix_rows, score_scale):
    return (
        jnp.einsum(
            "wjro,ujo->jrwu", query_matrix, key_matrix_rows, preferred_element_type=jnp.float32
        )
        * score_scale
    )


def decode_pair(
    query_matrix,
    own_keys,
    own_values,
    prompt_keys,
    prompt_values,
    valid_len,
    local_allowed,
    score_scale,
):
    key_slot_index = jnp.arange(prompt_keys.shape[0], dtype=jnp.int32)
    prompt_allowed = (key_slot_index < valid_len)[None, None, None, :]
    far_scores = pair_scores(query_matrix, prompt_keys, score_scale)
    near_scores = pair_scores(query_matrix, own_keys, score_scale)
    highest = jnp.maximum(
        masked_max(far_scores, prompt_allowed), masked_max(near_scores, local_allowed)
    )
    far_exp = jnp.where(prompt_allowed, jnp.exp(far_scores - highest), 0.0)
    near_exp = jnp.where(local_allowed, jnp.exp(near_scores - highest), 0.0)
    running = jnp.sum(far_exp, axis=-1, keepdims=True) + jnp.sum(near_exp, axis=-1, keepdims=True)
    return combine_values(far_exp / running, prompt_values) + combine_values(
        near_exp / running, own_values
    )


def plain_device(hidden, decode_hidden, norm_gain, qkv_weight, qkv_bias, lengths):
    prompt_count = lax.axis_size("grp")
    rep_count = lax.axis_size("rep")
    half_cycle = prompt_count // 2
    grp_here = lax.axis_index("grp")
    rep_here = lax.axis_index("rep")
    span_rows = hidden.shape[1]
    model_width = hidden.shape[2]
    head_block = (QPK + 2) * HD
    heads_here = qkv_bias.shape[0] // head_block
    decode_rows = decode_hidden.shape[3]
    score_scale = HD ** (-0.5)
    prefill_normed = normalize(hidden[0], norm_gain)
    decode_normed = normalize(decode_hidden.reshape(2 * decode_rows, model_width), norm_gain)
    normed = jnp.concatenate([prefill_normed, decode_normed], axis=0)
    share_cols = qkv_weight.shape[1] // rep_count
    own_cols = lax.dynamic_slice_in_dim(qkv_weight, rep_here * share_cols, share_cols, 1)
    columns = lax.all_gather(own_cols, "grp", axis=0, tiled=True)
    complete = lax.all_gather(columns, "rep", axis=1, tiled=True)
    projected = jnp.dot(normed, complete, preferred_element_type=jnp.float32)
    projected = (projected + qkv_bias.astype(jnp.float32)).reshape(
        normed.shape[0], heads_here, QPK + 2, HD
    )
    index_table = jnp.arange(prompt_count, dtype=jnp.int32)

    def length_of(prompt):
        return jnp.sum(jnp.where(index_table == prompt, lengths, 0))

    own_len = length_of(grp_here)
    far_len = length_of((grp_here + half_cycle) % prompt_count)
    row_position = rep_here * span_rows + jnp.arange(span_rows, dtype=jnp.int32)
    local_ids = jnp.arange(decode_rows, dtype=jnp.int32)
    step_ids = local_ids % STEPS
    sample_ids = local_ids // STEPS
    positions = jnp.concatenate([row_position, own_len + step_ids, far_len + step_ids])
    cosine, sine_part = rope_tables(positions, HD)
    query_matrix = rotate(
        projected[:, :, :QPK], cosine[:, None, None, :], sine_part[:, None, None, :]
    ).astype(jnp.bfloat16)
    key_matrix_rows = rotate(
        projected[:, :, QPK], cosine[:, None, :], sine_part[:, None, :]
    ).astype(jnp.bfloat16)
    value_matrix = projected[:, :, QPK + 1].astype(jnp.bfloat16)
    cache_keys, cache_values = (
        lax.all_gather(key_matrix_rows[:span_rows], "rep", axis=0, tiled=True),
        lax.all_gather(value_matrix[:span_rows], "rep", axis=0, tiled=True),
    )
    key_pos = jnp.arange(cache_keys.shape[0], dtype=jnp.int32)
    allowed = ((key_pos[None, :] <= row_position[:, None]) & (key_pos[None, :] < own_len))[
        None, None
    ]
    scores = pair_scores(query_matrix[:span_rows], cache_keys, score_scale)
    highest = masked_max(scores, allowed)
    exponent = jnp.where(allowed, jnp.exp(scores - highest), 0.0)
    weight_matrix = exponent / jnp.sum(exponent, axis=-1, keepdims=True)
    attended = combine_values(weight_matrix, cache_values)
    prefill_out = attended.astype(jnp.bfloat16).reshape(1, span_rows, heads_here * QPK * HD)
    decode_queries = query_matrix[span_rows:].reshape(2, decode_rows, heads_here, QPK, HD)
    decode_keys = key_matrix_rows[span_rows:].reshape(2, decode_rows, heads_here, HD)
    decode_values = value_matrix[span_rows:].reshape(2, decode_rows, heads_here, HD)
    local_allowed = (
        (sample_ids[None, :] == sample_ids[:, None]) & (step_ids[None, :] <= step_ids[:, None])
    )[None, None]
    near_out = decode_pair(
        decode_queries[0],
        decode_keys[0],
        decode_values[0],
        cache_keys,
        cache_values,
        own_len,
        local_allowed,
        score_scale,
    )
    far_keys, far_values = shifted((cache_keys, cache_values), "grp", half_cycle)
    far_out = decode_pair(
        decode_queries[1],
        decode_keys[1],
        decode_values[1],
        far_keys,
        far_values,
        far_len,
        local_allowed,
        score_scale,
    )
    decode_out = (
        jnp.stack([near_out, far_out])
        .astype(jnp.bfloat16)
        .reshape(1, 1, 2, decode_rows, heads_here * QPK * HD)
    )
    return (prefill_out, decode_out)


TILE = 512
MESH = pl.DeviceIdType.MESH


def gather_kernel(
    size, rows_up, hidden_ref, decode_ref, gain_ref, w_ref,
    acc_ref, wa_ref, wb_ref,
    x_ref, wt_ref, sa, ra, sb, rb, sx, rx, lx, lt,
):
    count = size
    depth = count // 2
    g = lax.axis_index("grp")
    r = lax.axis_index("rep")
    z = g // 2
    y = g % 2
    half = count // 2
    far = (g + half) % count
    span = hidden_ref.shape[1]
    drows = decode_ref.shape[3]
    share = w_ref.shape[0]
    cols_a = wa_ref.shape[2]
    cols_b = wb_ref.shape[2]
    tiles_a = cols_a // TILE
    rest = cols_a % TILE
    base = pl.multiple_of(r * (cols_a + cols_b), 128)
    base_b = pl.multiple_of(r * (cols_a + cols_b) + cols_a, 128)

    barrier = pltpu.get_barrier_semaphore()

    def greet(grp, rep):
        pl.semaphore_signal(barrier, inc=1, device_id={"grp": grp, "rep": rep}, device_id_type=MESH)

    greet(z * 2 + 1 - y, r)
    greet(g, 1 - r)
    greet(far, r)

    @pl.when(z >= 1)
    def _():
        greet(g - 2, r)

    @pl.when(z + 1 < depth)
    def _():
        greet(g + 2, r)

    inner = (z >= 1) & (z + 1 < depth)

    @pl.when(inner)
    def _():
        pl.semaphore_wait(barrier, 5)

    @pl.when(jnp.logical_not(inner))
    def _():
        pl.semaphore_wait(barrier, 4)

    def way(direction):
        return (g - 2, g + 2, z * 2 + 1 - y)[direction]

    def copy_a(o, direction, own):
        src = w_ref.at[:, pl.ds(base, cols_a)] if own else wa_ref.at[o]
        return pltpu.make_async_remote_copy(
            src, wa_ref.at[o], sa.at[o, direction], ra.at[o],
            device_id={"grp": way(direction)}, device_id_type=MESH,
        )

    def copy_b(o, direction, own):
        src = w_ref.at[:, pl.ds(base_b, cols_b)] if own else wb_ref.at[o]
        return pltpu.make_async_remote_copy(
            src, wb_ref.at[o], sb.at[o, direction], rb.at[o],
            device_id={"grp": way(direction)}, device_id_type=MESH,
        )

    def along(make, o, own, left, right):
        @pl.when(left)
        def _():
            make(o, 0, own).start()

        @pl.when(right)
        def _():
            make(o, 1, own).start()

    row_h = pl.multiple_of(r * span, 16)
    row_n = pl.multiple_of(2 * span + r * drows, 16)
    row_f = pl.multiple_of(2 * span + (2 + r) * drows, 16)
    row_o = pl.multiple_of(2 * span + (3 - r) * drows, 16)
    sib = {"rep": 1 - r}

    def send(src, row, n, i, device):
        return pltpu.make_async_remote_copy(
            src, x_ref.at[pl.ds(row, n), :], sx.at[i], rx.at[i], device_id=device, device_id_type=MESH
        )

    far_send = send(decode_ref.at[0, 0, 1], row_f, drows, 0, {"grp": far})
    far_send.start()
    along(copy_a, g, True, z >= 1, z + 1 < depth)
    copy_b(g, 2, True).start()
    copy_a(g, 2, True).start()
    hid_send = send(hidden_ref.at[0], row_h, span, 1, sib)
    near_send = send(decode_ref.at[0, 0, 0], row_n, drows, 2, sib)
    hid_send.start()
    near_send.start()
    own_h = pltpu.make_async_copy(hidden_ref.at[0], x_ref.at[pl.ds(row_h, span), :], lx.at[0])
    own_n = pltpu.make_async_copy(decode_ref.at[0, 0, 0], x_ref.at[pl.ds(row_n, drows), :], lx.at[1])
    own_h.start()
    own_n.start()

    @pl.loop(0, acc_ref.shape[0] // 16)
    def _(i):
        acc_ref[pl.ds(pl.multiple_of(i * 16, 16), 16), :] = jnp.zeros((16, acc_ref.shape[1]), jnp.float32)

    own_h.wait()
    own_n.wait()
    far_send.wait_recv()
    forward = send(x_ref.at[pl.ds(row_f, drows), :], row_f, drows, 3, sib)
    forward.start()
    hid_send.wait_recv()
    near_send.wait_recv()
    send(x_ref.at[pl.ds(row_o, drows), :], row_o, drows, 3, sib).wait_recv()
    forward.wait_send()
    gain = gain_ref[...].astype(jnp.float32)

    @pl.loop(0, x_ref.shape[0] // 16)
    def _(i):
        rows = pl.ds(pl.multiple_of(i * 16, 16), 16)
        wide = x_ref[rows, :].astype(jnp.float32)
        factor = lax.rsqrt(jnp.mean(wide * wide, axis=-1, keepdims=True) + EPSILON)
        x_ref[rows, :] = (wide * factor * gain).astype(jnp.bfloat16)

    def own_tile(off, n, slot_ref, sem):
        return pltpu.make_async_copy(w_ref.at[:, pl.ds(pl.multiple_of(base + off, 128), n)], slot_ref, sem)

    def add_product(o, slot, first):
        cols = pl.ds(pl.multiple_of(first, 128), TILE)
        acc_ref[:, cols] += jnp.dot(
            x_ref[:, pl.ds(pl.multiple_of(o * share, 128), share)], wt_ref[slot],
            preferred_element_type=jnp.float32,
        )

    def multiply(o):
        def fetch(t, slot):
            off = pl.multiple_of(t * TILE, 128)

            @pl.when(o == g)
            def _():
                own_tile(off, TILE, wt_ref.at[slot], lt.at[slot]).start()

            @pl.when(o != g)
            def _():
                pltpu.make_async_copy(wa_ref.at[o, :, pl.ds(off, TILE)], wt_ref.at[slot], lt.at[slot]).start()

        fetch(0, 0)

        @pl.loop(0, tiles_a)
        def _(t):
            slot = t % 2

            @pl.when(t + 1 < tiles_a)
            def _():
                fetch(t + 1, (t + 1) % 2)

            own_tile(0, TILE, wt_ref.at[slot], lt.at[slot]).wait()
            add_product(o, slot, t * TILE)

    def multiply_last(o):
        first = tiles_a * TILE

        @pl.when(o == g)
        def _():
            own_tile(first, TILE, wt_ref.at[0], lt.at[0]).start()
            own_tile(first, TILE, wt_ref.at[0], lt.at[0]).wait()

        @pl.when(o != g)
        def _():
            pieces = [pltpu.make_async_copy(wb_ref.at[o], wt_ref.at[0, :, pl.ds(rest, cols_b)], lt.at[0])]
            if rest:
                pieces.append(pltpu.make_async_copy(
                    wa_ref.at[o, :, pl.ds(first, rest)], wt_ref.at[0, :, pl.ds(0, rest)], lt.at[1]
                ))
            for piece in pieces:
                piece.start()
            for piece in pieces:
                piece.wait()

        add_product(o, 0, first)

    def arrive_b(k):
        for sign in (-1, 1):
            zz = z + sign * k

            @pl.when((zz >= 0) & (zz < depth))
            def _():
                for yy in (0, 1):
                    o = zz * 2 + yy
                    copy_b(o, 2, False).wait_recv()
                    if sign < 0:
                        along(copy_b, o, False, z < 0, z + 1 < depth)
                    else:
                        along(copy_b, o, False, z >= 1, z < 0)

    def multiply_b(low, high):
        @pl.loop(0, count)
        def _(o):
            hop = o // 2 - z

            @pl.when(((hop >= low) & (hop <= high)) | ((-hop >= low) & (-hop <= high)))
            def _():
                multiply_last(o)

    issue = max(1, depth - 2)

    @pl.loop(0, 4 * (depth + 1))
    def _(e):
        k = e // 4
        s = e % 4
        side = s // 2
        right = s % 2
        kk = k - side
        zz = z + (2 * right - 1) * kk
        yy = (y + side) % 2
        o = zz * 2 + yy

        @pl.when((k == issue) & (s == 2))
        def _():
            partner = z * 2 + 1 - y
            copy_b(partner, 2, False).wait_recv()
            along(copy_b, g, True, z >= 1, z + 1 < depth)
            along(copy_b, partner, False, z >= 1, z + 1 < depth)

        @pl.when((k == depth - 1) & (s == 2))
        def _():
            for hop in range(1, depth - 1):
                arrive_b(hop)

        @pl.when((k == depth) & (s == 0))
        def _():
            multiply_b(0, depth - 2)

        @pl.when((kk >= 0) & (zz >= 0) & (zz < depth) & ((kk > 0) | (right == 0)))
        def _():
            @pl.when(o != g)
            def _():
                copy_a(o, 2, False).wait_recv()

            @pl.when((side == 0) & (kk > 0))
            def _():
                along(copy_a, o, False, (right == 1) & (z >= 1), (right == 0) & (z + 1 < depth))
                copy_a(o, 2, False).start()

            multiply(o)

    arrive_b(depth - 1)
    multiply_b(depth - 1, depth - 1)

    far_send.wait_send()
    hid_send.wait_send()
    near_send.wait_send()

    @pl.loop(0, count)
    def _(o):
        zo = o // 2
        to_left = (zo >= z) & (z >= 1)
        to_right = (zo <= z) & (z + 1 < depth)

        @pl.when(o % 2 == y)
        def _():
            @pl.when(to_left)
            def _():
                copy_a(o, 0, False).wait_send()

            @pl.when(to_right)
            def _():
                copy_a(o, 1, False).wait_send()

            copy_a(o, 2, False).wait_send()

        @pl.when(to_left)
        def _():
            copy_b(o, 0, False).wait_send()

        @pl.when(to_right)
        def _():
            copy_b(o, 1, False).wait_send()

    copy_b(g, 2, False).wait_send()


def gather_project(hidden, decode_hidden, norm_gain, qkv_weight, reps):
    count = lax.axis_size("grp")
    rows = reps * (hidden.shape[1] + 2 * decode_hidden.shape[3])
    share = qkv_weight.shape[0]
    width = hidden.shape[2]
    cols = qkv_weight.shape[1] // reps
    cols_b = min(TILE, max(1, round(cols * 0.15 / 128)) * 128)
    cols_a = cols - cols_b
    hbm = pl.BlockSpec(memory_space=pl.ANY)
    vmem = pl.BlockSpec(memory_space=pltpu.VMEM)
    dma = pltpu.SemaphoreType.DMA
    return pl.pallas_call(
        functools.partial(gather_kernel, count, rows),
        out_shape=(
            jax.ShapeDtypeStruct((rows, cols), jnp.float32),
            jax.ShapeDtypeStruct((count, share, cols_a), jnp.bfloat16),
            jax.ShapeDtypeStruct((count, share, cols_b), jnp.bfloat16),
        ),
        in_specs=[hbm, hbm, vmem, hbm],
        out_specs=(vmem, hbm, hbm),
        scratch_shapes=[
            pltpu.VMEM((rows, width), jnp.bfloat16),
            pltpu.VMEM((2, share, TILE), jnp.bfloat16),
            dma((count, 3)), dma((count,)),
            dma((count, 3)), dma((count,)),
            dma((4,)), dma((4,)), dma((2,)), dma((2,)),
        ],
        compiler_params=pltpu.CompilerParams(
            collective_id=0, has_side_effects=True, vmem_limit_bytes=56 << 20
        ),
        name="gather_project",
    )(hidden, decode_hidden, norm_gain.reshape(1, width), qkv_weight)[0]


def attend_kernel(
    count, heads, block, len_ref, proj_ref, bias_ref, cos_ref, sin_ref, prefill_ref, decode_ref,
    q_ref, k_ref, v_ref, m_ref, out_ref, ss, rs, ls,
):
    rows = proj_ref.shape[0]
    h = pl.program_id(0)
    g = lax.axis_index("grp")
    r = lax.axis_index("rep")
    far = (g + count // 2) % count
    span = prefill_ref.shape[1]
    drows = decode_ref.shape[3]
    prompt_rows = rows - 4 * drows
    width = QPK * HD
    barrier = pltpu.get_barrier_semaphore()

    @pl.when(h == 0)
    def _():
        for grp, rep in ((g, 1 - r), (far, r), (far, 1 - r)):
            pl.semaphore_signal(barrier, inc=1, device_id={"grp": grp, "rep": rep}, device_id_type=MESH)

    def copies(i):
        cols = pl.ds(pl.multiple_of((r * heads + i) * width, 128), width)
        main = prefill_ref.at[0, :, cols]
        near = decode_ref.at[0, 0, 0, :, cols]
        away = decode_ref.at[0, 0, 1, :, cols]
        near_row = prompt_rows
        far_row = near_row + 2 * drows

        def piece(start, n):
            return out_ref.at[i, pl.ds(pl.multiple_of(start, 16), n), :]

        def send(src, dst, c, grp, rep):
            return pltpu.make_async_remote_copy(
                src, dst, ss.at[i, c], rs.at[i, c], device_id={"grp": grp, "rep": rep}, device_id_type=MESH
            )

        first = [
            send(piece(far_row + r * drows, drows), away, 0, far, r),
            send(piece(far_row + (1 - r) * drows, drows), away, 1, far, 1 - r),
            send(piece(near_row + (1 - r) * drows, drows), near, 3, g, 1 - r),
            pltpu.make_async_copy(piece(near_row + r * drows, drows), near, ls.at[i, 1]),
        ]
        second = [
            send(piece((1 - r) * span, span), main, 2, g, 1 - r),
            pltpu.make_async_copy(piece(r * span, span), main, ls.at[i, 0]),
        ]
        return first, second

    cosine = cos_ref[...]
    sine = sin_ref[...]
    factor = HD ** (-0.5) * math.log2(math.e)
    valid = len_ref[0]

    def part(j):
        cols = slice(j * HD, (j + 1) * HD)
        return proj_ref[:, cols] + bias_ref[:, cols]

    def turned(x):
        return x * cosine + pltpu.roll(x, HD // 2, 1) * sine

    for j in range(QPK):
        q_ref[j] = (turned(part(j)) * factor).astype(jnp.bfloat16)
    k_ref[...] = turned(part(QPK)).astype(jnp.bfloat16)
    v_ref[...] = part(QPK + 1).astype(jnp.bfloat16)

    def run(start, size, keys):
        shape = (size, keys)
        row = lax.broadcasted_iota(jnp.int32, shape, 0) + start
        col = lax.broadcasted_iota(jnp.int32, shape, 1)
        if start < prompt_rows:
            allowed = (col <= row) & (col < valid)
        else:
            same = ((row - prompt_rows) // STEPS == (col - prompt_rows) // STEPS) & (col <= row)
            allowed = (col < jnp.minimum(valid, prompt_rows)) | ((col >= prompt_rows) & same)
        m_ref[:size, :keys] = jnp.where(allowed, 0.0, NEGATIVE)

        for j in range(QPK):
            s = lax.dot_general(
                q_ref[j, start:start + size, :], k_ref[:keys, :], (((1,), (1,)), ((), ())),
                preferred_element_type=jnp.float32,
            ) + m_ref[:size, :keys]
            top = jnp.max(s, axis=-1, keepdims=True)
            p = jnp.exp2(s - top)
            total = jnp.sum(p, axis=-1, keepdims=True)
            o = jnp.dot(p.astype(jnp.bfloat16), v_ref[:keys, :], preferred_element_type=jnp.float32)
            out_ref[h, start:start + size, j * HD:(j + 1) * HD] = (o / total).astype(jnp.bfloat16)

    run(prompt_rows, rows - prompt_rows, rows)
    run(0, block, block)

    @pl.when(h == 0)
    def _():
        pl.semaphore_wait(barrier, 3)

    first, second = copies(h)
    for copy in first:
        copy.start()
    for start in range(block, prompt_rows, block):
        run(start, block, start + block)
    for copy in second:
        copy.start()

    @pl.when(h == heads - 1)
    def _():
        for i in range(heads):
            for part_copies in copies(i):
                for copy in part_copies:
                    copy.wait()


def attend(proj, bias_row, cosine, sine, valid, hidden, decode_hidden, reps):
    rows, cols = proj.shape
    head = (QPK + 2) * HD
    heads = cols // head
    prompt_rows = reps * hidden.shape[1]
    block = 256 if prompt_rows % 256 == 0 else prompt_rows
    size = max(block, rows - prompt_rows)
    width = reps * heads * QPK * HD
    dma = pltpu.SemaphoreType.DMA
    hbm = pl.BlockSpec(memory_space=pl.ANY)
    return pl.pallas_call(
        functools.partial(attend_kernel, lax.axis_size("grp"), heads, block),
        out_shape=(
            jax.ShapeDtypeStruct(hidden.shape[:2] + (width,), jnp.bfloat16),
            jax.ShapeDtypeStruct(decode_hidden.shape[:4] + (width,), jnp.bfloat16),
        ),
        grid=(heads,),
        in_specs=[
            pl.BlockSpec(memory_space=pltpu.SMEM),
            pl.BlockSpec((rows, head), lambda h: (0, h)),
            pl.BlockSpec((1, head), lambda h: (0, h)),
            pl.BlockSpec((rows, HD), lambda h: (0, 0)),
            pl.BlockSpec((rows, HD), lambda h: (0, 0)),
        ],
        out_specs=(hbm, hbm),
        scratch_shapes=[
            pltpu.VMEM((QPK, rows, HD), jnp.bfloat16),
            pltpu.VMEM((rows, HD), jnp.bfloat16),
            pltpu.VMEM((rows, HD), jnp.bfloat16),
            pltpu.VMEM((size, rows), jnp.float32),
            pltpu.VMEM((heads, rows, QPK * HD), jnp.bfloat16),
            dma((heads, 4)), dma((heads, 4)), dma((heads, 2)),
        ],
        compiler_params=pltpu.CompilerParams(
            collective_id=1, has_side_effects=True, vmem_limit_bytes=48 << 20
        ),
        name="attend",
    )(valid.reshape(1), proj, bias_row, cosine, sine)


def on_device(hidden, decode_hidden, norm_gain, qkv_weight, qkv_bias, lengths):
    count = lax.axis_size("grp")
    reps = lax.axis_size("rep")
    head_block = (QPK + 2) * HD
    heads_here = qkv_bias.shape[0] // head_block
    cols = qkv_weight.shape[1] // reps
    if reps != 2 or count % 2 or count < 4 or heads_here % reps or cols % TILE or cols < 2 * TILE or decode_hidden.shape[1] != 1:
        return plain_device(hidden, decode_hidden, norm_gain, qkv_weight, qkv_bias, lengths)
    g = lax.axis_index("grp")
    r = lax.axis_index("rep")
    half = count // 2
    span = hidden.shape[1]
    drows = decode_hidden.shape[3]
    prompt_rows = reps * span
    proj = gather_project(hidden, decode_hidden, norm_gain, qkv_weight, reps)

    index_table = jnp.arange(count, dtype=jnp.int32)
    own_len = jnp.sum(jnp.where(index_table == g, lengths, 0))
    steps = jnp.arange(2 * reps * drows, dtype=jnp.int32) % STEPS
    positions = jnp.concatenate([jnp.arange(prompt_rows, dtype=jnp.int32), own_len + steps])
    cosine, sine = rope_tables(positions, HD)
    cosine = jnp.concatenate([cosine, cosine], axis=-1)
    sine = jnp.concatenate([-sine, sine], axis=-1)
    bias_row = lax.dynamic_slice_in_dim(qkv_bias, r * cols, cols, 0).astype(jnp.float32).reshape(1, cols)
    return attend(proj, bias_row, cosine, sine, own_len, hidden, decode_hidden, reps)


def solution(mesh):
    return jax.shard_map(
        on_device,
        mesh=mesh,
        in_specs=(
            P("grp", "rep", None),
            P("grp", "rep", None, None, None),
            P(),
            P("grp", "tp"),
            P("tp"),
            P(),
        ),
        out_specs=(P("grp", "rep", "tp"), P("grp", "rep", None, None, "tp")),
        check_vma=False,
    )
```
